256 devices in a mesh: row: 16 (over x, y_hi, core), col: 16 (over y_lo, z).
Axes of the slice: x: 4, y: 4 (y_hi: 2, y_lo: 2; y = y_hi * 2 + y_lo), z: 8, core: 2. Of those that a mesh axis runs over, the one named last changes fastest.
Arguments:
- specimen_transmit: float32 [2, 2, 4096, 4096], P(None, None, 'row', 'col'), may hold values from -5 to 5
- illumination: float32 [2, 256, 256], replicated, may hold values from -5 to 5
- fresnel_angle: float32 [256, 256], replicated, may hold values from -3.140625 to 3.140625
- recorded_intensity: float32 [16, 16, 2, 256, 256], P('row', 'col'), may hold values from 0.1 to 3
- frame_shifts: int32 [16, 16, 2, 2], P('row', 'col'), may hold values from -128 to 128, as said below
Outputs:
- obj_grad: float32 [2, 2, 4096, 4096], P(None, None, 'row', 'col')
- probe_grad: float32 [2, 256, 256], P(None, 'row', 'col')
The draws below stay inside these ranges and needn't reach their ends.
Inputs may be any that keep to these rules, and one draw needn't show every extreme that they name: `frame_shifts`: shifts stay within the margin, so a window reaches only its own tile and the eight tiles around it; both ends of the range occur in every draw.
All inputs are finite; a program needn't handle non-finite values.
Results may differ from the reference program's by a relative error of at most 0.0003.
Values sent between devices are 32-bit elements; how exact they have to be, the bound alone decides.
No kernel may reach another device: no remote copies, remote signals or barrier semaphores. Data moves between devices by JAX's collectives and lax.ppermute only.
A program may use at most 128 MiB of HBM per device.

```python
import math
import jax
import jax.numpy as jnp
from jax import lax

FRAME_WIDTH = 256
HALO = 128
SLICES = 2
SCAN_STOPS = 2
TILE = 256
BRICKS_DOWN = 16
BRICKS_ACROSS = 16
NR = 4096
NC = 4096


def draw_frame_shifts(key, part):
    lowest = 0 - HALO
    highest = TILE + HALO - FRAME_WIDTH
    values = jax.random.randint(jax.random.fold_in(key, 11), (BRICKS_DOWN, BRICKS_ACROSS, SCAN_STOPS, 2), lowest, highest + 1)
    pick_rows = jax.random.randint(jax.random.fold_in(key, 12), (2,), 0, BRICKS_DOWN)
    pick_cols = jax.random.randint(jax.random.fold_in(key, 13), (2,), 0, BRICKS_ACROSS)
    values = values.at[pick_rows[0], pick_cols[0], 0, 0].set(lowest)
    values = values.at[pick_rows[1], pick_cols[1], SCAN_STOPS - 1, 1].set(highest)
    return values.astype(jnp.int32)


def block_scale(stream_key, shape, split, low, largest):
    level, own = 1.0, jax.random.fold_in(stream_key, 6)
    for position, blocks in split:
        draws = jnp.exp(jax.random.uniform(jax.random.fold_in(own, position), (blocks,), jnp.float32, low / len(split), largest / len(split)))
        level = level * jnp.repeat(draws, shape[position] // blocks).reshape([-1 if axis == position else 1 for axis in range(len(shape))])
    return level


def centred(stream_key, extent, scale, bound, split=(), held_as=jnp.bfloat16):
    gain = block_scale(stream_key, extent, split, -0.22, 0.18) if split else 1.0
    values = jax.random.normal(stream_key, extent, jnp.float32) * scale * gain
    return jnp.minimum(jnp.maximum(values, -bound), bound).astype(held_as)


def setup_inputs(seed: int = 0) -> dict:
    key_of = jax.random.split(jax.random.key(seed), 6)
    specimen_transmit = centred(key_of[0], (SLICES, 2, NR, NC), 0.7, 5.0, ((2, 16), (3, 16)), jnp.float32)
    illumination = centred(key_of[1], (2, FRAME_WIDTH, FRAME_WIDTH), 0.7, 5.0, (), jnp.float32)
    fresnel_angle = jnp.clip(jax.random.uniform(key_of[2], (FRAME_WIDTH, FRAME_WIDTH), jnp.float32, -3.140625, 3.140625), -3.140625, 3.140625)
    recorded_intensity = jnp.clip(jnp.exp(math.log(3.0) - 3.4011974 * jax.random.uniform(key_of[3], (BRICKS_DOWN, BRICKS_ACROSS, SCAN_STOPS, FRAME_WIDTH, FRAME_WIDTH), jnp.float32) ** block_scale(key_of[3], (BRICKS_DOWN, BRICKS_ACROSS, SCAN_STOPS, FRAME_WIDTH, FRAME_WIDTH), ((0, 16), (1, 16)), -0.2, 0.2)), 0.1, 3.0)
    frame_shifts = draw_frame_shifts(jax.random.fold_in(key_of[5], 71), 0)
    return dict(specimen_transmit=specimen_transmit, illumination=illumination, fresnel_angle=fresnel_angle, recorded_intensity=recorded_intensity, frame_shifts=frame_shifts)


def complex_product(a_real, a_imag, b_real, b_imag):
    return a_real * b_real - a_imag * b_imag, a_real * b_imag + a_imag * b_real


def conj_product(a_real, a_imag, b_real, b_imag):
    return a_real * b_real + a_imag * b_imag, a_real * b_imag - a_imag * b_real


def forward_dft(real_part, imag_part):
    result = jnp.fft.fft2(real_part + 1j * imag_part, norm="ortho")
    return jnp.real(result), jnp.imag(result)


def inverse_dft(real_part, imag_part):
    result = jnp.fft.ifft2(real_part + 1j * imag_part, norm="ortho")
    return jnp.real(result), jnp.imag(result)


def location_derivative(illuminated_frame, illumination, filter_inphase, filter_quadrature, observed_intensity):
    wave_real, wave_imag = illumination[0], illumination[1]
    saved = []
    for layer in range(SLICES):
        saved.append((wave_real, wave_imag))
        exit_real, exit_imag = complex_product(wave_real, wave_imag, illuminated_frame[layer, 0], illuminated_frame[layer, 1])
        if layer + 1 < SLICES:
            spec_real, spec_imag = forward_dft(exit_real, exit_imag)
            spec_real, spec_imag = complex_product(spec_real, spec_imag, filter_inphase, filter_quadrature)
            wave_real, wave_imag = inverse_dft(spec_real, spec_imag)
    far_real, far_imag = forward_dft(exit_real, exit_imag)
    misfit = far_real * far_real + far_imag * far_imag - observed_intensity
    back_real, back_imag = inverse_dft(misfit * far_real, misfit * far_imag)
    derivative_items = [None] * SLICES
    for layer in reversed(range(SLICES)):
        grad_real, grad_imag = conj_product(saved[layer][0], saved[layer][1], back_real, back_imag)
        derivative_items[layer] = jnp.stack([grad_real, grad_imag])
        head_real, head_imag = conj_product(illuminated_frame[layer, 0], illuminated_frame[layer, 1], back_real, back_imag)
        if layer > 0:
            spec_real, spec_imag = forward_dft(head_real, head_imag)
            spec_real, spec_imag = conj_product(filter_inphase, filter_quadrature, spec_real, spec_imag)
            back_real, back_imag = inverse_dft(spec_real, spec_imag)
    return jnp.stack(derivative_items), jnp.stack([head_real, head_imag])


def reference(specimen_transmit, illumination, fresnel_angle, recorded_intensity, frame_shifts):
    rows_total = specimen_transmit.shape[2]
    cols_total = specimen_transmit.shape[3]
    padded = jnp.pad(specimen_transmit, ((0, 0), (0, 0), (HALO, HALO), (HALO, HALO)), mode="wrap")
    filter_inphase = jnp.cos(fresnel_angle)
    filter_quadrature = jnp.sin(fresnel_angle)
    count = BRICKS_DOWN * BRICKS_ACROSS * SCAN_STOPS
    zero = jnp.zeros((), jnp.int32)

    def visit(carry, index):
        grad_pad, probe_sum = carry
        brick_down_number = index // (BRICKS_ACROSS * SCAN_STOPS)
        brick_across_number = (index // SCAN_STOPS) % BRICKS_ACROSS
        insert_frame = index % SCAN_STOPS
        shift = frame_shifts[brick_down_number, brick_across_number, insert_frame]
        start_row = (brick_down_number * TILE + shift[0] + HALO).astype(jnp.int32)
        start_col = (brick_across_number * TILE + shift[1] + HALO).astype(jnp.int32)
        illuminated_frame = lax.dynamic_slice(padded, (zero, zero, start_row, start_col), (SLICES, 2, FRAME_WIDTH, FRAME_WIDTH))
        derivative_items, incident_wave = location_derivative(illuminated_frame, illumination, filter_inphase, filter_quadrature, recorded_intensity[brick_down_number, brick_across_number, insert_frame])
        block = lax.dynamic_slice(grad_pad, (zero, zero, start_row, start_col), (SLICES, 2, FRAME_WIDTH, FRAME_WIDTH))
        grad_pad = lax.dynamic_update_slice(grad_pad, block + derivative_items, (zero, zero, start_row, start_col))
        return (grad_pad, probe_sum + incident_wave), None

    start = (jnp.zeros(padded.shape, specimen_transmit.dtype), jnp.zeros(illumination.shape, illumination.dtype))
    (grad_pad, probe_sum), _ = lax.scan(visit, start, jnp.arange(count, dtype=jnp.int32))
    core = grad_pad[:, :, HALO:HALO + rows_total, :]
    core = core.at[:, :, rows_total - HALO:, :].add(grad_pad[:, :, :HALO, :])
    core = core.at[:, :, :HALO, :].add(grad_pad[:, :, HALO + rows_total:, :])
    final = core[:, :, :, HALO:HALO + cols_total]
    final = final.at[:, :, :, cols_total - HALO:].add(core[:, :, :, :HALO])
    final = final.at[:, :, :, :HALO].add(core[:, :, :, HALO + cols_total:])
    return final, probe_sum
```

```python
import math

import jax
import jax.numpy as jnp
import numpy as np
from jax import lax
from jax.experimental import pallas as pl
from jax.experimental.pallas import tpu as pltpu
from jax.sharding import PartitionSpec as P

HALO = 128
TILE = 256
SIDE = TILE + 2 * HALO
PARTS = 4
F32 = jnp.float32
BF16 = jnp.bfloat16


def half_tables():
    n = np.arange(128)[:, None]
    out = []
    for odd in (0, 1):
        k = 2 * np.arange(128)[None, :] + odd
        angle = 2.0 * math.pi * ((n * k) % TILE) / TILE
        c, s = np.cos(angle) / 16.0, np.sin(angle) / 16.0
        whole = np.block([[c, -s], [s, c]]).astype(np.float32)
        for m in (whole, whole.T):
            high = m.astype(jnp.bfloat16)
            low = (m - high.astype(np.float32)).astype(jnp.bfloat16)
            out += [high, low]
    return np.stack(out)


EVEN, EVEN_T, ODD, ODD_T = 0, 2, 4, 6


def two(x):
    high = x.astype(BF16)
    return high, (x - high.astype(F32)).astype(BF16)


def dot(a, b):
    return jnp.dot(a, b, preferred_element_type=F32)


def right(x, tables, which):
    high, low = two(x)
    t, tl = tables[which], tables[which + 1]
    return dot(high, t) + (dot(low, t) + dot(high, tl))


def left(tables, which, x):
    high, low = two(x)
    t, tl = tables[which], tables[which + 1]
    return dot(t, high) + (dot(t, low) + dot(tl, high))


def rows(*parts):
    return jnp.concatenate(parts, axis=0)


def lanes(*parts):
    return jnp.concatenate(parts, axis=1)


def forward(re, im, tables):
    a = lanes(re[:, :128] + re[:, 128:], im[:, :128] + im[:, 128:])
    b = lanes(re[:, :128] - re[:, 128:], im[:, :128] - im[:, 128:])
    e = right(a, tables, EVEN)
    o = right(b, tables, ODD)
    pe, po = e[:128] + e[128:], o[:128] + o[128:]
    qe, qo = e[:128] - e[128:], o[:128] - o[128:]
    p = rows(lanes(pe[:, :128], po[:, :128]), lanes(pe[:, 128:], po[:, 128:]))
    q = rows(lanes(qe[:, :128], qo[:, :128]), lanes(qe[:, 128:], qo[:, 128:]))
    fe = left(tables, EVEN_T, p)
    fo = left(tables, ODD_T, q)
    return rows(fe[:128], fo[:128]), rows(fe[128:], fo[128:])


def inverse(re, im, tables):
    p = left(tables, EVEN, rows(re[:128], im[:128]))
    q = left(tables, ODD, rows(re[128:], im[128:]))
    top, bottom = p + q, p - q
    sr, si = rows(top[:128], bottom[:128]), rows(top[128:], bottom[128:])
    p = right(lanes(sr[:, :128], si[:, :128]), tables, EVEN_T)
    q = right(lanes(sr[:, 128:], si[:, 128:]), tables, ODD_T)
    u, v = p + q, p - q
    return lanes(u[:, :128], v[:, :128]), lanes(u[:, 128:], v[:, 128:])


def complex_product(a_real, a_imag, b_real, b_imag):
    return (a_real * b_real - a_imag * b_imag, a_real * b_imag + a_imag * b_real)


def conj_product(a_real, a_imag, b_real, b_imag):
    return (a_real * b_real + a_imag * b_imag, a_real * b_imag - a_imag * b_real)


OUTER, INNER, SIDE_A, SIDE_B, SHIFTS = 0, 1, 2, 3, 4


def at(where, which, back=0):
    return pl.multiple_of(where[which] - back, 128)


def pack_kernel(where, x, outer, side_a, side_b):
    outer[...] = x[:, pl.ds(pl.multiple_of(where[OUTER] // 3, 128), HALO), :]
    side_a[...] = x[:, :, pl.ds(pl.multiple_of(where[SIDE_A] // 3, 128), HALO)]
    side_b[...] = x[:, :, pl.ds(pl.multiple_of(where[SIDE_B] // 3, 128), HALO)]


def corner_kernel(where, outer, corner_a, corner_b):
    corner_a[...] = outer[:, :, pl.ds(pl.multiple_of(where[SIDE_A] // 3, 128), HALO)]
    corner_b[...] = outer[:, :, pl.ds(pl.multiple_of(where[SIDE_B] // 3, 128), HALO)]


def inner_kernel(where, x, got_a, got_b, inner):
    edge = pl.ds(pl.multiple_of(where[INNER] // 3, 128), HALO)
    inner[:, :, :TILE] = x[:, edge, :]
    inner[:, :, TILE : TILE + HALO] = got_a[:, edge, :]
    inner[:, :, TILE + HALO :] = got_b[:, edge, :]


def prepare_kernel(inphase, quadrature, intensity, out):
    i = lax.broadcasted_iota(jnp.int32, (TILE, TILE), 0)
    j = lax.broadcasted_iota(jnp.int32, (TILE, TILE), 1)
    pick = (i == jnp.where(j < 128, 2 * j, 2 * j - 255)).astype(F32)
    turn = (j == jnp.where(i < 128, 2 * i, 2 * i - 255)).astype(F32)

    def sort(x):
        x = jnp.dot(x, pick, precision=lax.Precision.HIGHEST, preferred_element_type=F32)
        return jnp.dot(turn, x, precision=lax.Precision.HIGHEST, preferred_element_type=F32)

    out[0] = sort(inphase[...])
    out[1] = sort(quadrature[...])
    out[2] = sort(intensity[0])
    out[3] = sort(intensity[1])


def main_kernel(
    where, x, outer, got_a, got_b, corner_a, corner_b, inner, probe, sorted_, tables,
    g_own, g_outer, g_a, g_b, g_corner_a, g_corner_b, g_inner, probe_out,
    ext, acc,
):
    own = pl.ds(HALO, TILE)
    o, i = pl.ds(at(where, OUTER), HALO), pl.ds(at(where, INNER), HALO)
    a, b = pl.ds(at(where, SIDE_A), HALO), pl.ds(at(where, SIDE_B), HALO)
    ext[:, own, own] = x[...]
    ext[:, o, own] = outer[...]
    ext[:, own, a] = got_a[...]
    ext[:, own, b] = got_b[...]
    ext[:, o, a] = corner_a[...]
    ext[:, o, b] = corner_b[...]
    ext[:, i, own] = inner[:, :, :TILE]
    ext[:, i, a] = inner[:, :, TILE : TILE + HALO]
    ext[:, i, b] = inner[:, :, TILE + HALO :]
    acc[...] = jnp.zeros_like(acc)
    filter_r, filter_i = sorted_[0], sorted_[1]
    probe_r, probe_i = probe[0], probe[1]
    total = None
    for p in range(2):
        start_row = where[SHIFTS + 2 * p] + HALO
        start_col = where[SHIFTS + 2 * p + 1] + HALO
        turn, step = lax.rem(start_col, 128), lax.rem(start_row, 8)
        place = (
            pl.ds(pl.multiple_of(start_row - step, 8), TILE + 8),
            pl.ds(pl.multiple_of(start_col - turn, 128), TILE + HALO),
        )

        def window(part):
            wide = ext[(part, *place)]
            wide = pltpu.roll(wide, lax.rem(TILE + HALO - turn, TILE + HALO), 1)[:, :TILE]
            return pltpu.roll(wide, lax.rem(TILE + 8 - step, TILE + 8), 0)[:TILE]

        def add(part, value):
            wide = lanes(value, jnp.zeros((TILE, HALO), F32))
            wide = pltpu.roll(wide, turn, 1)
            wide = rows(wide, jnp.zeros((8, TILE + HALO), F32))
            acc[(part, *place)] += pltpu.roll(wide, step, 0)

        x0 = window(0), window(1)
        e0 = complex_product(probe_r, probe_i, *x0)
        spec = complex_product(*forward(*e0, tables), filter_r, filter_i)
        psi = inverse(*spec, tables)
        x1 = window(2), window(3)
        e1 = complex_product(*psi, *x1)
        far_r, far_i = forward(*e1, tables)
        misfit = far_r * far_r + far_i * far_i - sorted_[2 + p]
        back = inverse(misfit * far_r, misfit * far_i, tables)
        for part, value in enumerate(conj_product(*psi, *back)):
            add(2 + part, value)
        h1 = conj_product(*x1, *back)
        spec = conj_product(filter_r, filter_i, *forward(*h1, tables))
        back = inverse(*spec, tables)
        for part, value in enumerate(conj_product(probe_r, probe_i, *back)):
            add(part, value)
        h0 = conj_product(*x0, *back)
        total = h0 if p == 0 else (total[0] + h0[0], total[1] + h0[1])
    for k in range(16):
        for part in range(2):
            probe_out[k, part] = total[part][16 * k : 16 * k + 16]
    g_own[...] = acc[:, own, own]
    g_outer[...] = acc[:, o, own]
    g_a[...] = acc[:, own, a]
    g_b[...] = acc[:, own, b]
    g_corner_a[...] = acc[:, o, a]
    g_corner_b[...] = acc[:, o, b]
    g_inner[:, :, :TILE] = acc[:, i, own]
    g_inner[:, :, TILE : TILE + HALO] = acc[:, i, a]
    g_inner[:, :, TILE + HALO :] = acc[:, i, b]


def sides_kernel(where, g_a, g_b, inner, side_a, side_b):
    edge = pl.ds(pl.multiple_of(where[INNER] // 3, 128), HALO)
    side_a[...] = g_a[...]
    side_b[...] = g_b[...]
    side_a[:, edge, :] += inner[:, :, TILE : TILE + HALO]
    side_b[:, edge, :] += inner[:, :, TILE + HALO :]


def outer_kernel(where, outer, corner_a, corner_b, out):
    out[...] = outer[...]
    out[:, :, pl.ds(pl.multiple_of(where[SIDE_A] // 3, 128), HALO)] += corner_a[...]
    out[:, :, pl.ds(pl.multiple_of(where[SIDE_B] // 3, 128), HALO)] += corner_b[...]


def final_kernel(where, own, inner, side_a, side_b, outer, out):
    out[...] = own[...]
    out[:, pl.ds(pl.multiple_of(where[INNER] // 3, 128), HALO), :] += inner[:, :, :TILE]
    out[:, :, pl.ds(pl.multiple_of(where[SIDE_A] // 3, 128), HALO)] += side_a[...]
    out[:, :, pl.ds(pl.multiple_of(where[SIDE_B] // 3, 128), HALO)] += side_b[...]
    out[:, pl.ds(pl.multiple_of(where[OUTER] // 3, 128), HALO), :] += outer[...]


def call(kernel, name, shapes, *operands, scalars=True, scratch=(), flops=0):
    smem = pl.BlockSpec(memory_space=pltpu.SMEM)
    vmem = pl.BlockSpec(memory_space=pltpu.VMEM)
    specs = [smem if scalars and k == 0 else vmem for k in range(len(operands))]
    size = sum(4 * math.prod(s) for s in shapes)
    return pl.pallas_call(
        kernel,
        name=name,
        out_shape=[jax.ShapeDtypeStruct(s, F32) for s in shapes],
        in_specs=specs,
        out_specs=[vmem] * len(shapes),
        scratch_shapes=list(scratch),
        cost_estimate=pl.CostEstimate(flops=flops, bytes_accessed=2 * size, transcendentals=0),
        compiler_params=pltpu.CompilerParams(vmem_limit_bytes=60 * 1024 * 1024),
    )(*operands)


NEAR = [(i, i ^ 1) for i in range(16)]
FAR = [(i, (i - 1 if i % 2 == 0 else i + 1) % 16) for i in range(16)]


def body(specimen_transmit, illumination, fresnel_angle, recorded_intensity, frame_shifts):
    row_odd = lax.axis_index("row") % 2
    col_odd = lax.axis_index("col") % 2
    outer_at, side_b_at = 384 * row_odd, 384 * col_odd
    where = jnp.concatenate(
        [
            jnp.stack([outer_at, 384 - outer_at, 384 - side_b_at, side_b_at]).astype(jnp.int32),
            frame_shifts.reshape(4),
        ]
    )
    x = specimen_transmit.reshape(PARTS, TILE, TILE)
    row_strip, col_strip = (PARTS, HALO, TILE), (PARTS, TILE, HALO)
    corner, wide_strip = (PARTS, HALO, HALO), (PARTS, HALO, SIDE)

    outer, side_a, side_b = call(pack_kernel, "pack", [row_strip, col_strip, col_strip], where, x)
    outer = lax.ppermute(outer, "row", FAR)
    got_a = lax.ppermute(side_a, "col", NEAR)
    got_b = lax.ppermute(side_b, "col", FAR)
    (ordered,) = call(
        prepare_kernel, "prepare", [(4, TILE, TILE)],
        jnp.cos(fresnel_angle), jnp.sin(fresnel_angle), recorded_intensity[0, 0],
        scalars=False, flops=300_000_000,
    )
    corner_a, corner_b = call(corner_kernel, "corner", [corner, corner], where, outer)
    corner_a = lax.ppermute(corner_a, "col", NEAR)
    corner_b = lax.ppermute(corner_b, "col", FAR)
    (inner,) = call(inner_kernel, "inner", [wide_strip], where, x, got_a, got_b)
    inner = lax.ppermute(inner, "row", NEAR)

    tables = jnp.asarray(half_tables())
    own, outer, side_a, side_b, corner_a, corner_b, inner, probe = call(
        main_kernel, "main",
        [(PARTS, TILE, TILE), row_strip, col_strip, col_strip, corner, corner, wide_strip,
         (16, 2, 16, TILE)],
        where, x, outer, got_a, got_b, corner_a, corner_b, inner, illumination, ordered, tables,
        scratch=[pltpu.VMEM((PARTS, SIDE + 8, SIDE + HALO), F32)] * 2, flops=5_000_000_000,
    )

    inner = lax.ppermute(inner, "row", NEAR)
    corner_a = lax.ppermute(corner_a, "col", NEAR)
    corner_b = lax.ppermute(corner_b, "col", FAR)
    side_a, side_b = call(sides_kernel, "sides", [col_strip] * 2, where, side_a, side_b, inner)
    side_a = lax.ppermute(side_a, "col", NEAR)
    side_b = lax.ppermute(side_b, "col", FAR)
    (outer,) = call(outer_kernel, "outer", [row_strip], where, outer, corner_a, corner_b)
    outer = lax.ppermute(outer, "row", FAR)
    (result,) = call(
        final_kernel, "final", [(PARTS, TILE, TILE)], where, own, inner, side_a, side_b, outer
    )

    probe = lax.all_to_all(probe, "row", 0, 0, tiled=True).sum(0)
    probe = probe.reshape(2, 16, 16, 16).transpose(2, 0, 1, 3)
    probe = lax.all_to_all(probe, "col", 0, 0, tiled=True).sum(0)
    return (result.reshape(specimen_transmit.shape), probe)


def solution(mesh):
    placed = (
        P(None, None, "row", "col"),
        P(),
        P(),
        P("row", "col", None, None, None),
        P("row", "col", None, None),
    )
    return jax.shard_map(
        body,
        mesh=mesh,
        in_specs=placed,
        out_specs=(P(None, None, "row", "col"), P(None, "row", "col")),
        check_vma=False,
    )
```

```python
import math

import jax
import jax.numpy as jnp
import numpy as np
from jax import lax
from jax.experimental import pallas as pl
from jax.experimental.pallas import tpu as pltpu
from jax.sharding import PartitionSpec as P


HALO = 128
TILE = 256
SIDE = TILE + 2 * HALO
PARTS = 4
F32 = jnp.float32
BF16 = jnp.bfloat16


def half_tables():
    n = np.arange(128)[:, None]
    out = []
    for odd in (0, 1):
        k = 2 * np.arange(128)[None, :] + odd
        angle = 2.0 * math.pi * ((n * k) % TILE) / TILE
        c, s = np.cos(angle) / 16.0, np.sin(angle) / 16.0
        whole = np.block([[c, -s], [s, c]]).astype(np.float32)
        for m in (whole, whole.T):
            high = m.astype(jnp.bfloat16)
            low = (m - high.astype(np.float32)).astype(jnp.bfloat16)
            out += [high, low]
    return np.stack(out)


EVEN, EVEN_T, ODD, ODD_T = 0, 2, 4, 6


def two(x):
    high = x.astype(BF16)
    return high, (x - high.astype(F32)).astype(BF16)


def dot(a, b):
    return jnp.dot(a, b, preferred_element_type=F32)


def right(x, tables, which):
    high, low = two(x)
    t, tl = tables[which], tables[which + 1]
    return dot(lanes(high, low, high), rows(t, t, tl))


def left(tables, which, x):
    high, low = two(x)
    t, tl = tables[which], tables[which + 1]
    return dot(lanes(t, t, tl), rows(high, low, high))


def rows(*parts):
    return jnp.concatenate(parts, axis=0)


def lanes(*parts):
    return jnp.concatenate(parts, axis=1)


def forward(re, im, tables):
    a = lanes(re[:, :128] + re[:, 128:], im[:, :128] + im[:, 128:])
    b = lanes(re[:, :128] - re[:, 128:], im[:, :128] - im[:, 128:])
    e = right(a, tables, EVEN)
    o = right(b, tables, ODD)
    pe, po = e[:128] + e[128:], o[:128] + o[128:]
    qe, qo = e[:128] - e[128:], o[:128] - o[128:]
    p = rows(lanes(pe[:, :128], po[:, :128]), lanes(pe[:, 128:], po[:, 128:]))
    q = rows(lanes(qe[:, :128], qo[:, :128]), lanes(qe[:, 128:], qo[:, 128:]))
    fe = left(tables, EVEN_T, p)
    fo = left(tables, ODD_T, q)
    return rows(fe[:128], fo[:128]), rows(fe[128:], fo[128:])


def inverse(re, im, tables):
    p = left(tables, EVEN, rows(re[:128], im[:128]))
    q = left(tables, ODD, rows(re[128:], im[128:]))
    top, bottom = p + q, p - q
    sr, si = rows(top[:128], bottom[:128]), rows(top[128:], bottom[128:])
    p = right(lanes(sr[:, :128], si[:, :128]), tables, EVEN_T)
    q = right(lanes(sr[:, 128:], si[:, 128:]), tables, ODD_T)
    u, v = p + q, p - q
    return lanes(u[:, :128], v[:, :128]), lanes(u[:, 128:], v[:, 128:])


def complex_product(a_real, a_imag, b_real, b_imag):
    return (a_real * b_real - a_imag * b_imag, a_real * b_imag + a_imag * b_real)


def conj_product(a_real, a_imag, b_real, b_imag):
    return (a_real * b_real + a_imag * b_imag, a_real * b_imag - a_imag * b_real)


OUTER, INNER, SIDE_A, SIDE_B = 0, 1, 2, 3


def at(where, which, back=0):
    return pl.multiple_of(where[which] - back, 128)


def pack_kernel(where, x, outer, side_a, side_b):
    outer[...] = x[:, pl.ds(pl.multiple_of(where[OUTER] // 3, 128), HALO), :]
    side_a[...] = x[:, :, pl.ds(pl.multiple_of(where[SIDE_A] // 3, 128), HALO)]
    side_b[...] = x[:, :, pl.ds(pl.multiple_of(where[SIDE_B] // 3, 128), HALO)]


def corner_kernel(where, outer, corner_a):
    corner_a[...] = outer[:, :, pl.ds(pl.multiple_of(where[SIDE_A] // 3, 128), HALO)]


def inner_kernel(where, x, got_a, got_b, inner, corner_b):
    edge = pl.ds(pl.multiple_of(where[INNER] // 3, 128), HALO)
    inner[:, :, :TILE] = x[:, edge, :]
    inner[:, :, TILE : TILE + HALO] = got_a[:, edge, :]
    inner[:, :, TILE + HALO :] = got_b[:, edge, :]
    corner_b[...] = got_b[:, pl.ds(pl.multiple_of(where[OUTER] // 3, 128), HALO), :]


def prepare_kernel(inphase, quadrature, intensity, out):
    i = lax.broadcasted_iota(jnp.int32, (TILE, TILE), 0)
    j = lax.broadcasted_iota(jnp.int32, (TILE, TILE), 1)
    pick = (i == jnp.where(j < 128, 2 * j, 2 * j - 255)).astype(F32)
    turn = (j == jnp.where(i < 128, 2 * i, 2 * i - 255)).astype(F32)

    def sort(x):
        x = jnp.dot(x, pick, precision=lax.Precision.HIGHEST, preferred_element_type=F32)
        return jnp.dot(turn, x, precision=lax.Precision.HIGHEST, preferred_element_type=F32)

    out[0] = sort(inphase[...])
    out[1] = sort(quadrature[...])
    out[2] = sort(intensity[0])
    out[3] = sort(intensity[1])


def main_kernel(
    where, shifts, x, outer, got_a, got_b, corner_a, corner_b, inner, probe, sorted_, tables,
    g_own, g_outer, g_a, g_b, g_corner_a, g_corner_b, g_inner, probe_out,
    ext, acc,
):
    own = pl.ds(HALO, TILE)
    o, i = pl.ds(at(where, OUTER), HALO), pl.ds(at(where, INNER), HALO)
    a, b = pl.ds(at(where, SIDE_A), HALO), pl.ds(at(where, SIDE_B), HALO)
    ext[:, own, own] = x[...]
    ext[:, o, own] = outer[...]
    ext[:, own, a] = got_a[...]
    ext[:, own, b] = got_b[...]
    ext[:, o, a] = corner_a[...]
    ext[:, o, b] = corner_b[...]
    ext[:, i, own] = inner[:, :, :TILE]
    ext[:, i, a] = inner[:, :, TILE : TILE + HALO]
    ext[:, i, b] = inner[:, :, TILE + HALO :]
    acc[...] = jnp.zeros_like(acc)
    filter_r, filter_i = sorted_[0], sorted_[1]
    probe_r, probe_i = probe[0], probe[1]
    places, turns, steps = [], [], []
    for p in range(2):
        start_row = shifts[0, 0, p, 0] + HALO
        start_col = shifts[0, 0, p, 1] + HALO
        turn, step = lax.rem(start_col, 128), lax.rem(start_row, 8)
        turns.append(turn)
        steps.append(step)
        places.append(
            (
                pl.ds(pl.multiple_of(start_row - step, 8), TILE + 8),
                pl.ds(pl.multiple_of(start_col - turn, 128), TILE + HALO),
            )
        )

    def window(p, part):
        wide = ext[(part, *places[p])]
        wide = pltpu.roll(wide, lax.rem(TILE + HALO - turns[p], TILE + HALO), 1)[:, :TILE]
        return pltpu.roll(wide, lax.rem(TILE + 8 - steps[p], TILE + 8), 0)[:TILE]

    def add(p, part, value):
        wide = lanes(value, jnp.zeros((TILE, HALO), F32))
        wide = pltpu.roll(wide, turns[p], 1)
        wide = rows(wide, jnp.zeros((8, TILE + HALO), F32))
        acc[(part, *places[p])] += pltpu.roll(wide, steps[p], 0)

    both = (0, 1)
    x0 = [(window(p, 0), window(p, 1)) for p in both]
    e0 = [complex_product(probe_r, probe_i, *x0[p]) for p in both]
    spec = [complex_product(*forward(*e0[p], tables), filter_r, filter_i) for p in both]
    psi = [inverse(*spec[p], tables) for p in both]
    x1 = [(window(p, 2), window(p, 3)) for p in both]
    e1 = [complex_product(*psi[p], *x1[p]) for p in both]
    far = [forward(*e1[p], tables) for p in both]
    back = []
    for p in both:
        far_r, far_i = far[p]
        misfit = far_r * far_r + far_i * far_i - sorted_[2 + p]
        back.append(inverse(misfit * far_r, misfit * far_i, tables))
    for p in both:
        for part, value in enumerate(conj_product(*psi[p], *back[p])):
            add(p, 2 + part, value)
    h1 = [conj_product(*x1[p], *back[p]) for p in both]
    spec = [conj_product(filter_r, filter_i, *forward(*h1[p], tables)) for p in both]
    back = [inverse(*spec[p], tables) for p in both]
    for p in both:
        for part, value in enumerate(conj_product(probe_r, probe_i, *back[p])):
            add(p, part, value)
    h0 = [conj_product(*x0[p], *back[p]) for p in both]
    total = h0[0][0] + h0[1][0], h0[0][1] + h0[1][1]
    for k in range(16):
        for part in range(2):
            probe_out[k, part] = total[part][16 * k : 16 * k + 16]
    g_own[...] = acc[:, own, own]
    g_outer[...] = acc[:, o, own]
    g_a[...] = acc[:, own, a]
    g_b[...] = acc[:, own, b]
    g_corner_a[...] = acc[:, o, a]
    g_corner_b[...] = acc[:, o, b]
    g_inner[:, :, :TILE] = acc[:, i, own]
    g_inner[:, :, TILE : TILE + HALO] = acc[:, i, a]
    g_inner[:, :, TILE + HALO :] = acc[:, i, b]


def sides_kernel(where, g_a, g_b, inner, side_a, side_b):
    edge = pl.ds(pl.multiple_of(where[INNER] // 3, 128), HALO)
    side_a[...] = g_a[...]
    side_b[...] = g_b[...]
    side_a[:, edge, :] += inner[:, :, TILE : TILE + HALO]
    side_b[:, edge, :] += inner[:, :, TILE + HALO :]


def outer_kernel(where, outer, corner_a, corner_b, out):
    out[...] = outer[...]
    out[:, :, pl.ds(pl.multiple_of(where[SIDE_A] // 3, 128), HALO)] += corner_a[...]
    out[:, :, pl.ds(pl.multiple_of(where[SIDE_B] // 3, 128), HALO)] += corner_b[...]


def final_kernel(where, own, inner, side_a, side_b, outer, out):
    out[...] = own[...]
    out[:, pl.ds(pl.multiple_of(where[INNER] // 3, 128), HALO), :] += inner[:, :, :TILE]
    out[:, :, pl.ds(pl.multiple_of(where[SIDE_A] // 3, 128), HALO)] += side_a[...]
    out[:, :, pl.ds(pl.multiple_of(where[SIDE_B] // 3, 128), HALO)] += side_b[...]
    out[:, pl.ds(pl.multiple_of(where[OUTER] // 3, 128), HALO), :] += outer[...]


def strip_kernel(got, out):
    total = got[0]
    for k in range(1, 16):
        total = total + got[k]
    tall = rows(total[0], total[1], jnp.zeros((96, TILE), F32)).T
    for k in range(16):
        quads = [tall[16 * k + 4 * j : 16 * k + 4 * j + 4, :32] for j in range(4)]
        out[k] = lanes(*quads)


def patch_kernel(got, out):
    total = got[0]
    for k in range(1, 16):
        total = total + got[k]
    quads = [total[:, 32 * j : 32 * j + 32] for j in range(4)]
    wide = lanes(rows(*quads), jnp.zeros((16, 96), F32))
    tall = rows(wide, jnp.zeros((112, 128), F32)).T
    out[0] = tall[:16, :16]
    out[1] = tall[16:32, :16]


def call(kernel, shapes, *operands, scalars=1, scratch=(), flops=0, grant=6, hbm=False):
    smem = pl.BlockSpec(memory_space=pltpu.SMEM)
    vmem = pl.BlockSpec(memory_space=pltpu.VMEM)
    specs = [smem if k < scalars else vmem for k in range(len(operands))]
    size = sum(4 * math.prod(s) for s in shapes)
    return pl.pallas_call(
        kernel,
        out_shape=[pltpu.HBM(s, F32) if hbm else jax.ShapeDtypeStruct(s, F32) for s in shapes],
        in_specs=specs,
        out_specs=[vmem] * len(shapes),
        scratch_shapes=list(scratch),
        cost_estimate=pl.CostEstimate(flops=flops, bytes_accessed=2 * size, transcendentals=0),
        compiler_params=pltpu.CompilerParams(vmem_limit_bytes=grant * 1024 * 1024),
    )(*operands)


NEAR = [(i, i ^ 1) for i in range(16)]
FAR = [(i, (i - 1 if i % 2 == 0 else i + 1) % 16) for i in range(16)]


def body(specimen_transmit, illumination, fresnel_angle, recorded_intensity, frame_shifts):
    row_odd = lax.axis_index("row") % 2
    col_odd = lax.axis_index("col") % 2
    outer_at, side_b_at = 384 * row_odd, 384 * col_odd
    where = jnp.stack([outer_at, 384 - outer_at, 384 - side_b_at, side_b_at]).astype(jnp.int32)
    x = specimen_transmit.reshape(PARTS, TILE, TILE)
    row_strip, col_strip = (PARTS, HALO, TILE), (PARTS, TILE, HALO)
    corner, wide_strip = (PARTS, HALO, HALO), (PARTS, HALO, SIDE)

    outer, side_a, side_b = call(pack_kernel, [row_strip, col_strip, col_strip], where, x)
    outer = lax.ppermute(outer, "row", FAR)
    got_b = lax.ppermute(side_b, "col", FAR)
    got_a = lax.ppermute(side_a, "col", NEAR)
    (ordered,) = call(
        prepare_kernel, [(4, TILE, TILE)],
        jnp.cos(fresnel_angle), jnp.sin(fresnel_angle), recorded_intensity[0, 0],
        scalars=0, flops=300_000_000,
    )
    (corner_a,) = call(corner_kernel, [corner], where, outer)
    corner_a = lax.ppermute(corner_a, "col", NEAR)
    inner, corner_b = call(inner_kernel, [wide_strip, corner], where, x, got_a, got_b)
    corner_b = lax.ppermute(corner_b, "row", FAR)
    inner = lax.ppermute(inner, "row", NEAR)

    tables = jnp.asarray(half_tables())
    own, outer, side_a, side_b, corner_a, corner_b, inner, probe = call(
        main_kernel,
        [(PARTS, TILE, TILE), row_strip, col_strip, col_strip, corner, corner, wide_strip,
         (16, 2, 16, TILE)],
        where, frame_shifts, x, outer, got_a, got_b, corner_a, corner_b, inner, illumination,
        ordered, tables, scalars=2,
        scratch=[pltpu.VMEM((PARTS, SIDE + 8, SIDE + HALO), F32)] * 2, flops=5_000_000_000, grant=26,
        hbm=True,
    )

    inner = lax.ppermute(inner, "row", NEAR)
    corner_b = lax.ppermute(corner_b, "col", FAR)
    corner_a = lax.ppermute(corner_a, "col", NEAR)
    side_a, side_b = call(sides_kernel, [col_strip] * 2, where, side_a, side_b, inner)
    side_a = lax.ppermute(side_a, "col", NEAR)
    side_b = lax.ppermute(side_b, "col", FAR)
    (outer,) = call(outer_kernel, [row_strip], where, outer, corner_a, corner_b)
    outer = lax.ppermute(outer, "row", FAR)
    (result,) = call(final_kernel, [(PARTS, TILE, TILE)], where, own, inner, side_a, side_b, outer)

    probe = lax.all_to_all(probe, "row", 0, 0, tiled=True)
    (probe,) = call(strip_kernel, [(16, 4, 128)], probe, scalars=0, grant=4)
    probe = lax.all_to_all(probe, "col", 0, 0, tiled=True)
    (probe,) = call(patch_kernel, [(2, 16, 16)], probe, scalars=0, grant=4)
    return (result.reshape(specimen_transmit.shape), probe)


def solution(mesh):
    placed = (
        P(None, None, "row", "col"),
        P(),
        P(),
        P("row", "col", None, None, None),
        P("row", "col", None, None),
    )
    return jax.shard_map(
        body,
        mesh=mesh,
        in_specs=placed,
        out_specs=(P(None, None, "row", "col"), P(None, "row", "col")),
        check_vma=False,
    )
```

```python
import math

import jax
import jax.numpy as jnp
import numpy as np
from jax import lax
from jax.experimental import pallas as pl
from jax.experimental.pallas import tpu as pltpu
from jax.sharding import PartitionSpec as P


HALO = 128
TILE = 256
SIDE = TILE + 2 * HALO
PARTS = 4
F32 = jnp.float32
BF16 = jnp.bfloat16


def half_tables():
    n = np.arange(128)[:, None]
    out = []
    for odd in (0, 1):
        k = 2 * np.arange(128)[None, :] + odd
        angle = 2.0 * math.pi * ((n * k) % TILE) / TILE
        c, s = np.cos(angle) / 16.0, np.sin(angle) / 16.0
        whole = np.block([[c, -s], [s, c]]).astype(np.float32)
        for m in (whole, whole.T):
            high = m.astype(jnp.bfloat16)
            low = (m - high.astype(np.float32)).astype(jnp.bfloat16)
            out += [high, low]
    return np.stack(out)


EVEN, EVEN_T, ODD, ODD_T = 0, 2, 4, 6


def two(x):
    high = x.astype(BF16)
    return high, (x - high.astype(F32)).astype(BF16)


def dot(a, b):
    return jnp.dot(a, b, preferred_element_type=F32)


def right(x, tables, which):
    high, low = two(x)
    t, tl = tables[which], tables[which + 1]
    return dot(lanes(high, low, high), rows(t, t, tl))


def left(tables, which, x):
    high, low = two(x)
    t, tl = tables[which], tables[which + 1]
    return dot(lanes(t, t, tl), rows(high, low, high))


def rows(*parts):
    return jnp.concatenate(parts, axis=0)


def lanes(*parts):
    return jnp.concatenate(parts, axis=1)


def forward(re, im, tables):
    a = lanes(re[:, :128] + re[:, 128:], im[:, :128] + im[:, 128:])
    b = lanes(re[:, :128] - re[:, 128:], im[:, :128] - im[:, 128:])
    e = right(a, tables, EVEN)
    o = right(b, tables, ODD)
    pe, po = e[:128] + e[128:], o[:128] + o[128:]
    qe, qo = e[:128] - e[128:], o[:128] - o[128:]
    p = rows(lanes(pe[:, :128], po[:, :128]), lanes(pe[:, 128:], po[:, 128:]))
    q = rows(lanes(qe[:, :128], qo[:, :128]), lanes(qe[:, 128:], qo[:, 128:]))
    fe = left(tables, EVEN_T, p)
    fo = left(tables, ODD_T, q)
    return rows(fe[:128], fo[:128]), rows(fe[128:], fo[128:])


def inverse(re, im, tables):
    p = left(tables, EVEN, rows(re[:128], im[:128]))
    q = left(tables, ODD, rows(re[128:], im[128:]))
    top, bottom = p + q, p - q
    sr, si = rows(top[:128], bottom[:128]), rows(top[128:], bottom[128:])
    p = right(lanes(sr[:, :128], si[:, :128]), tables, EVEN_T)
    q = right(lanes(sr[:, 128:], si[:, 128:]), tables, ODD_T)
    u, v = p + q, p - q
    return lanes(u[:, :128], v[:, :128]), lanes(u[:, 128:], v[:, 128:])


def complex_product(a_real, a_imag, b_real, b_imag):
    return (a_real * b_real - a_imag * b_imag, a_real * b_imag + a_imag * b_real)


def conj_product(a_real, a_imag, b_real, b_imag):
    return (a_real * b_real + a_imag * b_imag, a_real * b_imag - a_imag * b_real)


OUTER, INNER, SIDE_A, SIDE_B = 0, 1, 2, 3


def at(where, which, back=0):
    return pl.multiple_of(where[which] - back, 128)


def pack_kernel(where, x, outer, side_a, side_b):
    outer[...] = x[:, pl.ds(pl.multiple_of(where[OUTER] // 3, 128), HALO), :]
    side_a[...] = x[:, :, pl.ds(pl.multiple_of(where[SIDE_A] // 3, 128), HALO)]
    side_b[...] = x[:, :, pl.ds(pl.multiple_of(where[SIDE_B] // 3, 128), HALO)]


def corner_kernel(where, outer, corner_a):
    corner_a[...] = outer[:, :, pl.ds(pl.multiple_of(where[SIDE_A] // 3, 128), HALO)]


def inner_kernel(where, x, got_a, got_b, inner, corner_b):
    edge = pl.ds(pl.multiple_of(where[INNER] // 3, 128), HALO)
    inner[:, :, :TILE] = x[:, edge, :]
    inner[:, :, TILE : TILE + HALO] = got_a[:, edge, :]
    inner[:, :, TILE + HALO :] = got_b[:, edge, :]
    corner_b[...] = got_b[:, pl.ds(pl.multiple_of(where[OUTER] // 3, 128), HALO), :]


def prepare_kernel(inphase, quadrature, intensity, out):
    i = lax.broadcasted_iota(jnp.int32, (TILE, TILE), 0)
    j = lax.broadcasted_iota(jnp.int32, (TILE, TILE), 1)
    pick = (i == jnp.where(j < 128, 2 * j, 2 * j - 255)).astype(F32)
    turn = (j == jnp.where(i < 128, 2 * i, 2 * i - 255)).astype(F32)

    def sort(x):
        x = jnp.dot(x, pick, precision=lax.Precision.HIGHEST, preferred_element_type=F32)
        return jnp.dot(turn, x, precision=lax.Precision.HIGHEST, preferred_element_type=F32)

    out[0] = sort(inphase[...])
    out[1] = sort(quadrature[...])
    out[2] = sort(intensity[0])
    out[3] = sort(intensity[1])


def main_kernel(
    where, shifts, x, outer, got_a, got_b, corner_a, corner_b, inner, probe, sorted_, tables,
    g_own, g_outer, g_a, g_b, g_corner_a, g_corner_b, g_inner, probe_out,
    ext, acc,
):
    own = pl.ds(HALO, TILE)
    o, i = pl.ds(at(where, OUTER), HALO), pl.ds(at(where, INNER), HALO)
    a, b = pl.ds(at(where, SIDE_A), HALO), pl.ds(at(where, SIDE_B), HALO)
    ext[:, own, own] = x[...]
    ext[:, o, own] = outer[...]
    ext[:, own, a] = got_a[...]
    ext[:, own, b] = got_b[...]
    ext[:, o, a] = corner_a[...]
    ext[:, o, b] = corner_b[...]
    ext[:, i, own] = inner[:, :, :TILE]
    ext[:, i, a] = inner[:, :, TILE : TILE + HALO]
    ext[:, i, b] = inner[:, :, TILE + HALO :]
    acc[...] = jnp.zeros_like(acc)
    filter_r, filter_i = sorted_[0], sorted_[1]
    probe_r, probe_i = probe[0], probe[1]
    places, turns, steps = [], [], []
    for p in range(2):
        start_row = shifts[0, 0, p, 0] + HALO
        start_col = shifts[0, 0, p, 1] + HALO
        turn, step = lax.rem(start_col, 128), lax.rem(start_row, 8)
        turns.append(turn)
        steps.append(step)
        places.append(
            (
                pl.ds(pl.multiple_of(start_row - step, 8), TILE + 8),
                pl.ds(pl.multiple_of(start_col - turn, 128), TILE + HALO),
            )
        )

    def window(p, part):
        wide = ext[(part, *places[p])]
        wide = pltpu.roll(wide, lax.rem(TILE + HALO - turns[p], TILE + HALO), 1)[:, :TILE]
        return pltpu.roll(wide, lax.rem(TILE + 8 - steps[p], TILE + 8), 0)[:TILE]

    def add(p, part, value):
        wide = lanes(value, jnp.zeros((TILE, HALO), F32))
        wide = pltpu.roll(wide, turns[p], 1)
        wide = rows(wide, jnp.zeros((8, TILE + HALO), F32))
        acc[(part, *places[p])] += pltpu.roll(wide, steps[p], 0)

    both = (0, 1)
    x0 = [(window(p, 0), window(p, 1)) for p in both]
    e0 = [complex_product(probe_r, probe_i, *x0[p]) for p in both]
    spec = [complex_product(*forward(*e0[p], tables), filter_r, filter_i) for p in both]
    psi = [inverse(*spec[p], tables) for p in both]
    x1 = [(window(p, 2), window(p, 3)) for p in both]
    e1 = [complex_product(*psi[p], *x1[p]) for p in both]
    far = [forward(*e1[p], tables) for p in both]
    back = []
    for p in both:
        far_r, far_i = far[p]
        misfit = far_r * far_r + far_i * far_i - sorted_[2 + p]
        back.append(inverse(misfit * far_r, misfit * far_i, tables))
    for p in both:
        for part, value in enumerate(conj_product(*psi[p], *back[p])):
            add(p, 2 + part, value)
    h1 = [conj_product(*x1[p], *back[p]) for p in both]
    spec = [conj_product(filter_r, filter_i, *forward(*h1[p], tables)) for p in both]
    back = [inverse(*spec[p], tables) for p in both]
    for p in both:
        for part, value in enumerate(conj_product(probe_r, probe_i, *back[p])):
            add(p, part, value)
    h0 = [conj_product(*x0[p], *back[p]) for p in both]
    total = h0[0][0] + h0[1][0], h0[0][1] + h0[1][1]
    for k in range(16):
        for part in range(2):
            probe_out[k, part] = total[part][16 * k : 16 * k + 16]
    g_own[...] = acc[:, own, own]
    g_outer[...] = acc[:, o, own]
    g_a[...] = acc[:, own, a]
    g_b[...] = acc[:, own, b]
    g_corner_a[...] = acc[:, o, a]
    g_corner_b[...] = acc[:, o, b]
    g_inner[:, :, :TILE] = acc[:, i, own]
    g_inner[:, :, TILE : TILE + HALO] = acc[:, i, a]
    g_inner[:, :, TILE + HALO :] = acc[:, i, b]


def sides_kernel(where, g_a, g_b, inner, side_a, side_b):
    edge = pl.ds(pl.multiple_of(where[INNER] // 3, 128), HALO)
    side_a[...] = g_a[...]
    side_b[...] = g_b[...]
    side_a[:, edge, :] += inner[:, :, TILE : TILE + HALO]
    side_b[:, edge, :] += inner[:, :, TILE + HALO :]


def outer_kernel(where, outer, corner_a, corner_b, out):
    out[...] = outer[...]
    out[:, :, pl.ds(pl.multiple_of(where[SIDE_A] // 3, 128), HALO)] += corner_a[...]
    out[:, :, pl.ds(pl.multiple_of(where[SIDE_B] // 3, 128), HALO)] += corner_b[...]


def final_kernel(where, own, inner, side_a, side_b, outer, out):
    out[...] = own[...]
    out[:, pl.ds(pl.multiple_of(where[INNER] // 3, 128), HALO), :] += inner[:, :, :TILE]
    out[:, :, pl.ds(pl.multiple_of(where[SIDE_A] // 3, 128), HALO)] += side_a[...]
    out[:, :, pl.ds(pl.multiple_of(where[SIDE_B] // 3, 128), HALO)] += side_b[...]
    out[:, pl.ds(pl.multiple_of(where[OUTER] // 3, 128), HALO), :] += outer[...]


def strip_kernel(got, out):
    total = got[0]
    for k in range(1, 16):
        total = total + got[k]
    tall = rows(total[0], total[1], jnp.zeros((96, TILE), F32)).T
    for k in range(16):
        quads = [tall[16 * k + 4 * j : 16 * k + 4 * j + 4, :32] for j in range(4)]
        out[k] = lanes(*quads)


def patch_kernel(got, out):
    total = got[0]
    for k in range(1, 16):
        total = total + got[k]
    quads = [total[:, 32 * j : 32 * j + 32] for j in range(4)]
    wide = lanes(rows(*quads), jnp.zeros((16, 96), F32))
    tall = rows(wide, jnp.zeros((112, 128), F32)).T
    out[0] = tall[:16, :16]
    out[1] = tall[16:32, :16]


def call(kernel, shapes, *operands, scalars=1, scratch=(), flops=0, grant=6, hbm=False, planes=False):
    smem = pl.BlockSpec(memory_space=pltpu.SMEM)
    vmem = pl.BlockSpec(memory_space=pltpu.VMEM)
    specs = [smem if k < scalars else vmem for k in range(len(operands))]
    outs, grid = [vmem] * len(shapes), ()
    if planes:
        grid = (PARTS,)
        plane = lambda s: pl.BlockSpec((1, *s[1:]), lambda k: (k, 0, 0))
        specs = [smem] + [plane(x.shape) for x in operands[1:]]
        outs = [plane(s) for s in shapes]
    size = sum(4 * math.prod(s) for s in shapes)
    return pl.pallas_call(
        kernel,
        out_shape=[pltpu.HBM(s, F32) if hbm else jax.ShapeDtypeStruct(s, F32) for s in shapes],
        in_specs=specs,
        out_specs=outs,
        grid=grid,
        scratch_shapes=list(scratch),
        cost_estimate=pl.CostEstimate(flops=flops, bytes_accessed=2 * size, transcendentals=0),
        compiler_params=pltpu.CompilerParams(vmem_limit_bytes=grant * 1024 * 1024),
    )(*operands)


NEAR = [(i, i ^ 1) for i in range(16)]
FAR = [(i, (i - 1 if i % 2 == 0 else i + 1) % 16) for i in range(16)]


def body(specimen_transmit, illumination, fresnel_angle, recorded_intensity, frame_shifts):
    row_odd = lax.axis_index("row") % 2
    col_odd = lax.axis_index("col") % 2
    outer_at, side_b_at = 384 * row_odd, 384 * col_odd
    where = jnp.stack([outer_at, 384 - outer_at, 384 - side_b_at, side_b_at]).astype(jnp.int32)
    x = specimen_transmit.reshape(PARTS, TILE, TILE)
    row_strip, col_strip = (PARTS, HALO, TILE), (PARTS, TILE, HALO)
    corner, wide_strip = (PARTS, HALO, HALO), (PARTS, HALO, SIDE)

    outer, side_a, side_b = call(pack_kernel, [row_strip, col_strip, col_strip], where, x)
    outer = lax.ppermute(outer, "row", FAR)
    got_b = lax.ppermute(side_b, "col", FAR)
    got_a = lax.ppermute(side_a, "col", NEAR)
    (ordered,) = call(
        prepare_kernel, [(4, TILE, TILE)],
        jnp.cos(fresnel_angle), jnp.sin(fresnel_angle), recorded_intensity[0, 0],
        scalars=0, flops=300_000_000,
    )
    (corner_a,) = call(corner_kernel, [corner], where, outer)
    corner_a = lax.ppermute(corner_a, "col", NEAR)
    inner, corner_b = call(inner_kernel, [wide_strip, corner], where, x, got_a, got_b)
    corner_b = lax.ppermute(corner_b, "row", FAR)
    inner = lax.ppermute(inner, "row", NEAR)

    tables = jnp.asarray(half_tables())
    own, outer, side_a, side_b, corner_a, corner_b, inner, probe = call(
        main_kernel,
        [(PARTS, TILE, TILE), row_strip, col_strip, col_strip, corner, corner, wide_strip,
         (16, 2, 16, TILE)],
        where, frame_shifts, x, outer, got_a, got_b, corner_a, corner_b, inner, illumination,
        ordered, tables, scalars=2,
        scratch=[pltpu.VMEM((PARTS, SIDE + 8, SIDE + HALO), F32)] * 2, flops=5_000_000_000, grant=26,
        hbm=True,
    )

    inner = lax.ppermute(inner, "row", NEAR)
    corner_b = lax.ppermute(corner_b, "col", FAR)
    corner_a = lax.ppermute(corner_a, "col", NEAR)
    side_a, side_b = call(sides_kernel, [col_strip] * 2, where, side_a, side_b, inner, planes=True)
    side_a = lax.ppermute(side_a, "col", NEAR)
    side_b = lax.ppermute(side_b, "col", FAR)
    (outer,) = call(outer_kernel, [row_strip], where, outer, corner_a, corner_b, planes=True)
    outer = lax.ppermute(outer, "row", FAR)
    (result,) = call(
        final_kernel, [(PARTS, TILE, TILE)], where, own, inner, side_a, side_b, outer,
        planes=True,
    )

    probe = lax.all_to_all(probe, "row", 0, 0, tiled=True)
    (probe,) = call(strip_kernel, [(16, 4, 128)], probe, scalars=0, grant=4)
    probe = lax.all_to_all(probe, "col", 0, 0, tiled=True)
    (probe,) = call(patch_kernel, [(2, 16, 16)], probe, scalars=0, grant=4)
    return (result.reshape(specimen_transmit.shape), probe)


def solution(mesh):
    placed = (
        P(None, None, "row", "col"),
        P(),
        P(),
        P("row", "col", None, None, None),
        P("row", "col", None, None),
    )
    return jax.shard_map(
        body,
        mesh=mesh,
        in_specs=placed,
        out_specs=(P(None, None, "row", "col"), P(None, "row", "col")),
        check_vma=False,
    )
```
